32 devices in a mesh: lat: 4 (over y, x), lon: 8 (over z, core).
Axes of the slice: x: 2, y: 2, z: 4, core: 2. Of those that a mesh axis runs over, the one named last changes fastest.
Arguments:
- patches: bfloat16 [128, 256, 1280], P('lat', 'lon'), may hold values from -6 to 6
- w_embed: bfloat16 [1280, 1024], replicated, may hold values from -0.15625 to 0.15625
- b_embed: float32 [1024], replicated, may hold values from -2 to 2
- pos_embed: bfloat16 [128, 256, 1024], P('lat', 'lon'), may hold values from -3 to 3
- gain_one: float32 [1024], replicated, may hold values from 0.1 to 1.9
- shift_one: float32 [1024], replicated, may hold values from -2 to 2
- w_spec_one: bfloat16 [2, 8, 128, 128], replicated, may hold values from -0.375 to 0.375
- b_spec_one: float32 [2, 8, 128], replicated, may hold values from -2 to 2
- w_spec_two: bfloat16 [2, 8, 128, 128], replicated, may hold values from -0.375 to 0.375
- b_spec_two: float32 [2, 8, 128], replicated, may hold values from -2 to 2
- gain_two: float32 [1024], replicated, may hold values from 0.1 to 1.9
- shift_two: float32 [1024], replicated, may hold values from -2 to 2
- w_fc_one: bfloat16 [1024, 4096], replicated, may hold values from -0.1875 to 0.1875
- b_fc_one: float32 [4096], replicated, may hold values from -2 to 2
- w_fc_two: bfloat16 [4096, 1024], replicated, may hold values from -0.09375 to 0.09375
- b_fc_two: float32 [1024], replicated, may hold values from -2 to 2
Outputs:
- block_out: bfloat16 [128, 256, 1024], P('lat', 'lon')
The draws below stay inside these ranges and needn't reach their ends.
All inputs are finite; a program needn't handle non-finite values.
Results may differ from the reference program's by a relative error of at most 0.01.
Values may be sent and summed in bfloat16 or wider, within the bound.
A program may use at most 128 MiB of HBM per device.

```python
import math
import jax
import jax.numpy as jnp
from jax import lax

D = 1024
HID = 4096
NB = 8
PIN = 1280
BS = 128
H = 128
W = 256
KW = 128


def block_levels(own_key, dims, split, low, largest):
    def one(position, shards_of):
        heights = jax.random.uniform(jax.random.fold_in(jax.random.fold_in(own_key, 6), position), (shards_of,), jnp.float32, low / len(split), largest / len(split))
        return jnp.repeat(jnp.exp(heights), dims[position] // shards_of).reshape((-1,) + (1,) * (len(dims) - position - 1))

    level = one(*split[0])
    for cut in split[1:]:
        level = level * one(*cut)
    return level


def normal_values(stream_key, shape, width, most, pieces=(), held_as=jnp.bfloat16):
    level = block_levels(stream_key, shape, pieces, -0.22, 0.18) if pieces else 1.0
    array = jax.random.normal(stream_key, shape, jnp.float32) * width * level
    return jnp.minimum(jnp.maximum(array, -most), most).astype(held_as)


def setup_inputs(seed: int = 0) -> dict:
    arg_keys = jax.random.split(jax.random.key(seed), 17)
    return {
        "patches": normal_values(arg_keys[0], (H, W, PIN), 1.0, 6.0, ((0, 4), (1, 8))),
        "w_embed": normal_values(arg_keys[1], (PIN, D), PIN ** -0.5, 0.15625),
        "b_embed": normal_values(arg_keys[2], (D,), 0.3, 2.0, (), jnp.float32),
        "pos_embed": normal_values(arg_keys[3], (H, W, D), 0.5, 3.0, ((0, 4), (1, 8))),
        "gain_one": jnp.clip(1.0 + 0.18 * jax.random.normal(arg_keys[4], (D,), jnp.float32), 0.1, 1.9),
        "shift_one": normal_values(arg_keys[5], (D,), 0.3, 2.0, (), jnp.float32),
        "w_spec_one": normal_values(arg_keys[6], (2, NB, BS, BS), (2 * BS) ** -0.5, 0.375),
        "b_spec_one": normal_values(arg_keys[7], (2, NB, BS), 0.3, 2.0, (), jnp.float32),
        "w_spec_two": normal_values(arg_keys[8], (2, NB, BS, BS), (2 * BS) ** -0.5, 0.375),
        "b_spec_two": normal_values(arg_keys[9], (2, NB, BS), 0.3, 2.0, (), jnp.float32),
        "gain_two": jnp.clip(1.0 + 0.18 * jax.random.normal(arg_keys[10], (D,), jnp.float32), 0.1, 1.9),
        "shift_two": normal_values(arg_keys[11], (D,), 0.3, 2.0, (), jnp.float32),
        "w_fc_one": normal_values(arg_keys[12], (D, HID), D ** -0.5, 0.1875),
        "b_fc_one": normal_values(arg_keys[13], (HID,), 0.3, 2.0, (), jnp.float32),
        "w_fc_two": normal_values(arg_keys[14], (HID, D), HID ** -0.5, 0.09375),
        "b_fc_two": normal_values(arg_keys[15], (D,), 0.3, 2.0, (), jnp.float32),
    }


def angle_table(length, mode_count):
    product = jnp.arange(mode_count, dtype=jnp.int32)[:, None] * jnp.arange(length, dtype=jnp.int32)[None, :] % length
    phase = product.astype(jnp.float32) * (2.0 * math.pi / length)
    return (jnp.cos(phase), jnp.sin(phase))

def layer_norm(values, gain_vec, shift_vec):
    floats = values.astype(jnp.float32)
    center = lax.optimization_barrier(jnp.mean(floats, axis=-1, keepdims=True))
    spread = lax.optimization_barrier(jnp.mean(jnp.square(floats - center), axis=-1, keepdims=True))
    return (floats - center) * lax.rsqrt(spread + 1e-06) * gain_vec + shift_vec

def shrink(values):
    return jnp.where(values > 0.01, values - 0.01, jnp.where(values < -0.01, values + 0.01, jnp.zeros_like(values)))

def contract(table, field, form):
    return jnp.einsum(form, table.astype(jnp.float32), field.astype(jnp.float32))

def block_mix(real_part, imag_part, weights):
    left = real_part.astype(jnp.float32)
    right = imag_part.astype(jnp.float32)
    wre = weights[0].astype(jnp.float32)
    wim = weights[1].astype(jnp.float32)
    form = 'hkbi,bio->hkbo'
    out_re = jnp.einsum(form, left, wre) - jnp.einsum(form, right, wim)
    out_im = jnp.einsum(form, left, wim) + jnp.einsum(form, right, wre)
    return (out_re, out_im)

def reference(patches, w_embed, b_embed, pos_embed, gain_one, shift_one, w_spec_one, b_spec_one, w_spec_two, b_spec_two, gain_two, shift_two, w_fc_one, b_fc_one, w_fc_two, b_fc_two):
    flat = jnp.dot(patches.reshape(H * W, PIN), w_embed, preferred_element_type=jnp.float32)
    embedded = (flat + b_embed + pos_embed.reshape(H * W, D).astype(jnp.float32)).astype(jnp.bfloat16).reshape(H, W, D)
    normed = layer_norm(embedded, gain_one, shift_one).astype(jnp.bfloat16)
    scale = 1.0 / math.sqrt(H * W)
    cos_w, sin_w = angle_table(W, KW)
    fwd_cos = cos_w.T.astype(jnp.bfloat16)
    fwd_sin = (-sin_w).T.astype(jnp.bfloat16)
    lon_re = contract(fwd_cos, normed, 'wk,hwd->hkd').astype(jnp.bfloat16)
    lon_im = contract(fwd_sin, normed, 'wk,hwd->hkd').astype(jnp.bfloat16)
    cos_h, sin_h = angle_table(H, H)
    cos_h = cos_h.astype(jnp.bfloat16)
    sin_h = sin_h.astype(jnp.bfloat16)
    form = 'qh,hkd->qkd'
    spec_re = (scale * (contract(cos_h, lon_re, form) + contract(sin_h, lon_im, form))).astype(jnp.bfloat16)
    spec_im = (scale * (contract(cos_h, lon_im, form) - contract(sin_h, lon_re, form))).astype(jnp.bfloat16)
    spec_re = spec_re.reshape(H, KW, NB, BS)
    spec_im = spec_im.reshape(H, KW, NB, BS)
    mix_re, mix_im = block_mix(spec_re, spec_im, w_spec_one)
    first_re = jax.nn.relu(mix_re + b_spec_one[0]).astype(jnp.bfloat16)
    first_im = jax.nn.relu(mix_im + b_spec_one[1]).astype(jnp.bfloat16)
    mix_re, mix_im = block_mix(first_re, first_im, w_spec_two)
    shrunk_re = shrink(mix_re + b_spec_two[0]).astype(jnp.bfloat16).reshape(H, KW, D)
    shrunk_im = shrink(mix_im + b_spec_two[1]).astype(jnp.bfloat16).reshape(H, KW, D)
    back_re = (contract(cos_h, shrunk_re, form) - contract(sin_h, shrunk_im, form)).astype(jnp.bfloat16)
    back_im = (contract(sin_h, shrunk_re, form) + contract(cos_h, shrunk_im, form)).astype(jnp.bfloat16)
    weight_k = jnp.where(jnp.arange(KW, dtype=jnp.int32) == 0, 1.0, 2.0).astype(jnp.float32)[:, None]
    inv_cos = (weight_k * cos_w).astype(jnp.bfloat16)
    inv_sin = (weight_k * sin_w).astype(jnp.bfloat16)
    filtered = (scale * (contract(inv_cos, back_re, 'kw,hkd->hwd') - contract(inv_sin, back_im, 'kw,hkd->hwd'))).astype(jnp.bfloat16)

    def finish_row(items):
        filt_row, norm_row, embed_row = items
        mixed = (filt_row.astype(jnp.float32) + norm_row.astype(jnp.float32) + embed_row.astype(jnp.float32)).astype(jnp.bfloat16)
        normed_two = layer_norm(mixed, gain_two, shift_two).astype(jnp.bfloat16)
        hidden = jax.nn.gelu(jnp.dot(normed_two, w_fc_one, preferred_element_type=jnp.float32) + b_fc_one, approximate=False).astype(jnp.bfloat16)
        result = mixed.astype(jnp.float32) + jnp.dot(hidden, w_fc_two, preferred_element_type=jnp.float32) + b_fc_two
        return result.astype(jnp.bfloat16)
    return lax.map(finish_row, (filtered, normed, embedded))
```

```python
import functools
import math

import jax
import jax.numpy as jnp
import numpy as np
from jax import lax
from jax.experimental import pallas as pl
from jax.experimental.pallas import tpu as pltpu
from jax.sharding import PartitionSpec as P

MESH = pl.DeviceIdType.MESH
FORWARD_CHUNKS = 8
BACK_CHUNKS = 4
AHEAD = 3


def angle_table(length, mode_count):
    product = (
        jnp.arange(mode_count, dtype=jnp.int32)[:, None]
        * jnp.arange(length, dtype=jnp.int32)[None, :]
        % length
    )
    phase = product.astype(jnp.float32) * (2.0 * math.pi / length)
    return (jnp.cos(phase), jnp.sin(phase))


def layer_norm(values, gain_vec, shift_vec):
    floats = values.astype(jnp.float32)
    center = jnp.mean(floats, axis=-1, keepdims=True)
    spread = jnp.mean(jnp.square(floats - center), axis=-1, keepdims=True)
    return (floats - center) * lax.rsqrt(spread + 1e-06) * gain_vec + shift_vec


def shrink(values):
    return jnp.where(
        values > 0.01,
        values - 0.01,
        jnp.where(values < -0.01, values + 0.01, jnp.zeros_like(values)),
    )


def contract(table, field, form):
    return jnp.einsum(form, table, field, preferred_element_type=jnp.float32)


def block_mix(real_part, imag_part, weights):
    form = "nbi,bio->nbo"
    out_re = contract(real_part, weights[0], form) - contract(imag_part, weights[1], form)
    out_im = contract(real_part, weights[1], form) + contract(imag_part, weights[0], form)
    return (out_re, out_im)


def host_tables(length, mode_count):
    product = np.arange(mode_count)[:, None] * np.arange(length)[None, :] % length
    phase = product.astype(np.float32) * np.float32(2.0 * math.pi / length)
    return (np.cos(phase).astype(np.float32), np.sin(phase).astype(np.float32))


def norm_rows(values, gain_row, shift_row):
    floats = values.astype(jnp.float32)
    center = jnp.mean(floats, axis=-1, keepdims=True)
    floats = floats - center
    spread = jnp.mean(floats * floats, axis=-1, keepdims=True)
    return floats * lax.rsqrt(spread + 1e-06) * gain_row + shift_row


def dot(left, right):
    return jnp.dot(left, right, preferred_element_type=jnp.float32)


def fused_kernel(
    lat_count,
    lon_count,
    patches,
    w_embed,
    b_embed,
    pos_embed,
    gain_one,
    shift_one,
    w_spec_one,
    b_spec_one,
    w_spec_two,
    b_spec_two,
    gain_two,
    shift_two,
    w_fc_one,
    b_fc_one,
    w_fc_two,
    b_fc_two,
    lon_table,
    lon_back,
    lat_table,
    lat_back,
    out,
    patches_v,
    w_embed_v,
    pos_v,
    w_fc_one_v,
    w_fc_two_v,
    embedded,
    normed,
    circles,
    waves,
    columns,
    modes,
    back,
    cycles,
    filtered,
    tokens_in,
    total,
    result,
    in_sem,
    out_sem,
    s1,
    r1,
    s2,
    r2,
    s3,
    r3,
    s4,
    r4,
):
    tile_rows, tile_cols, patch_len = patches_v.shape
    width = w_embed_v.shape[1]
    chans = circles.shape[3]
    total_rows = tile_rows * lat_count
    total_cols = tile_cols * lon_count
    pair = columns.shape[2]
    own_waves = pair // 2
    pitch = modes.shape[0] // total_rows
    scale = 1.0 / math.sqrt(total_rows * total_cols)
    my_lat = lax.axis_index("lat")
    my_lon = lax.axis_index("lon")
    half = lon_count // 2
    lon_steps = sorted(range(1, lon_count), key=lambda d: abs(d - half))
    lat_steps = list(range(1, lat_count))

    def lon_peer(step):
        return lax.rem(my_lon + step, lon_count)

    def lat_peer(step):
        return lax.rem(my_lat + step, lat_count)

    def fetch(source, target, index):
        return pltpu.make_async_copy(source, target, in_sem.at[index])

    first_copies = [
        fetch(w_embed, w_embed_v, 0),
        fetch(patches, patches_v, 1),
        fetch(pos_embed, pos_v, 2),
    ]
    later_copies = [fetch(w_fc_one, w_fc_one_v, 3), fetch(w_fc_two, w_fc_two_v, 4)]
    for copy in first_copies:
        copy.start()

    barrier = pltpu.get_barrier_semaphore()
    for step in lon_steps:
        pl.semaphore_signal(
            barrier, inc=1, device_id={"lon": lon_peer(step)}, device_id_type=MESH
        )
    for step in lat_steps:
        pl.semaphore_signal(
            barrier, inc=1, device_id={"lat": lat_peer(step)}, device_id_type=MESH
        )
    pl.semaphore_wait(barrier, lon_count + lat_count - 2)

    def exchange(axis, send, recv, send_sem, recv_sem, chunk, rows, peer, mine):
        return pltpu.make_async_remote_copy(
            src_ref=send.at[peer, rows],
            dst_ref=recv.at[mine, rows],
            send_sem=send_sem.at[chunk, peer],
            recv_sem=recv_sem.at[chunk, mine],
            device_id={axis: peer},
            device_id_type=MESH,
        )

    def lon_send(send, recv, send_sem, recv_sem, chunk, rows):
        for step in lon_steps:
            exchange(
                "lon", send, recv, send_sem, recv_sem, chunk, rows, lon_peer(step), my_lon
            ).start()

    def lat_send(send, recv, send_sem, recv_sem, chunk, rows):
        for step in lat_steps:
            exchange(
                "lat", send, recv, send_sem, recv_sem, chunk, rows, lat_peer(step), my_lat
            ).start()

    def lon_arrive(send, recv, send_sem, recv_sem, chunk, rows):
        for step in lon_steps:
            peer = lon_peer(step)
            exchange("lon", send, recv, send_sem, recv_sem, chunk, rows, peer, peer).wait_recv()

    def lat_arrive(send, recv, send_sem, recv_sem, chunk, rows):
        for step in lat_steps:
            peer = lat_peer(step)
            exchange("lat", send, recv, send_sem, recv_sem, chunk, rows, peer, peer).wait_recv()

    def sent(axis, steps, peer_of, mine, send, recv, send_sem, recv_sem, chunk, rows):
        for step in steps:
            exchange(
                axis, send, recv, send_sem, recv_sem, chunk, rows, peer_of(step), mine
            ).wait_send()

    front = (normed, circles, s1, r1)
    over = (waves, columns, s2, r2)
    under = (back, cycles, s3, r3)
    home = (filtered, tokens_in, s4, r4)
    fwd_rows = tile_rows // FORWARD_CHUNKS
    back_rows = tile_rows // BACK_CHUNKS

    for copy in first_copies:
        copy.wait()
    for copy in later_copies:
        copy.start()

    @pl.loop(0, FORWARD_CHUNKS)
    def embed_step(chunk):
        rows = pl.ds(chunk * fwd_rows, fwd_rows)
        count = fwd_rows * tile_cols
        flat = dot(patches_v[rows].reshape(count, patch_len), w_embed_v[...])
        flat = flat + b_embed[...] + pos_v[rows].reshape(count, width).astype(jnp.float32)
        rounded = flat.astype(jnp.bfloat16)
        embedded[rows] = rounded.reshape(fwd_rows, tile_cols, width)
        scaled = norm_rows(rounded, gain_one[...], shift_one[...]).astype(jnp.bfloat16)
        for block in range(lon_count):
            piece = scaled[:, block * chans : (block + 1) * chans]
            normed[block, rows] = piece.reshape(fwd_rows, tile_cols, chans)
        lon_send(*front, chunk, rows)
        circles[my_lon, rows] = normed[my_lon, rows]

    @pl.loop(0, FORWARD_CHUNKS)
    def wave_step(chunk):
        rows = pl.ds(chunk * fwd_rows, fwd_rows)
        lon_arrive(*front, chunk, rows)
        for row in range(0, fwd_rows, 2):
            base = chunk * fwd_rows + row
            field = jnp.concatenate(
                [circles[:, base + i].reshape(total_cols, chans) for i in range(2)], axis=1
            )
            spectrum = dot(lon_table[...], field).astype(jnp.bfloat16)
            for owner in range(lat_count):
                for i in range(2):
                    waves[owner, base + i] = spectrum[
                        owner * pair : (owner + 1) * pair, i * chans : (i + 1) * chans
                    ]
        lat_send(*over, chunk, rows)
        columns[my_lat, rows] = waves[my_lat, rows]

    @pl.loop(0, FORWARD_CHUNKS)
    def widen_step(chunk):
        rows = pl.ds(chunk * fwd_rows, fwd_rows)
        lat_arrive(*over, chunk, rows)
        for owner in range(lat_count):
            for row in range(fwd_rows):
                place = (owner * tile_rows + chunk * fwd_rows + row) * pitch
                modes[pl.ds(pl.multiple_of(place, 8), pair), :] = columns[
                    owner, chunk * fwd_rows + row
                ].astype(jnp.float32)

    def mix_matrix(weights):
        real, imag = weights[0, my_lon], weights[1, my_lon]
        return jnp.concatenate(
            [
                jnp.concatenate([real, imag], axis=1),
                jnp.concatenate([-imag, real], axis=1),
            ],
            axis=0,
        )

    def mix_bias(bias):
        return jnp.concatenate(
            [bias[0, pl.ds(my_lon, 1), :], bias[1, pl.ds(my_lon, 1), :]], axis=1
        )

    mix_one, mix_two = mix_matrix(w_spec_one), mix_matrix(w_spec_two)
    bias_one, bias_two = mix_bias(b_spec_one), mix_bias(b_spec_two)
    group = 8

    @pl.loop(0, own_waves // group)
    def mode_step(step):
        def place(i, part):
            return pl.ds(step * group + i + part * own_waves, total_rows, stride=pitch)

        field = jnp.concatenate(
            [
                jnp.concatenate([modes[place(i, 0), :], modes[place(i, 1), :]], axis=0).astype(
                    jnp.bfloat16
                )
                for i in range(group)
            ],
            axis=1,
        )
        spec = (scale * dot(lat_table[...], field)).astype(jnp.bfloat16)
        stacked = jnp.concatenate(
            [
                jnp.concatenate(
                    [
                        spec[:total_rows, i * chans : (i + 1) * chans],
                        spec[total_rows:, i * chans : (i + 1) * chans],
                    ],
                    axis=1,
                )
                for i in range(group)
            ],
            axis=0,
        )
        first = jnp.maximum(dot(stacked, mix_one) + bias_one, 0.0).astype(jnp.bfloat16)
        second = shrink(dot(first, mix_two) + bias_two).astype(jnp.bfloat16)
        turned = jnp.concatenate(
            [
                jnp.concatenate(
                    [
                        second[i * total_rows : (i + 1) * total_rows, :chans],
                        second[i * total_rows : (i + 1) * total_rows, chans:],
                    ],
                    axis=0,
                )
                for i in range(group)
            ],
            axis=1,
        )
        returned = dot(lat_back[...], turned)
        for i in range(group):
            modes[place(i, 0), :] = returned[:total_rows, i * chans : (i + 1) * chans]
            modes[place(i, 1), :] = returned[total_rows:, i * chans : (i + 1) * chans]

    @pl.loop(0, BACK_CHUNKS)
    def return_step(chunk):
        rows = pl.ds(chunk * back_rows, back_rows)
        for owner in range(lat_count):
            for row in range(back_rows):
                place = (owner * tile_rows + chunk * back_rows + row) * pitch
                back[owner, chunk * back_rows + row] = modes[
                    pl.ds(pl.multiple_of(place, 8), pair), :
                ].astype(jnp.bfloat16)
        lat_send(*under, chunk, rows)
        cycles[my_lat, rows] = back[my_lat, rows]

    def inverse_step(chunk):
        rows = pl.ds(chunk * back_rows, back_rows)
        lat_arrive(*under, chunk, rows)
        for row in range(0, back_rows, 2):
            base = chunk * back_rows + row
            field = jnp.concatenate(
                [cycles[:, base + i].reshape(lat_count * pair, chans) for i in range(2)], axis=1
            )
            values = (scale * dot(lon_back[...], field)).astype(jnp.bfloat16)
            for owner in range(lon_count):
                for i in range(2):
                    filtered[owner, base + i] = values[
                        owner * tile_cols : (owner + 1) * tile_cols, i * chans : (i + 1) * chans
                    ]
        lon_send(*home, chunk, rows)
        tokens_in[my_lon, rows] = filtered[my_lon, rows]

    @pl.loop(0, AHEAD)
    def inverse_ahead(chunk):
        inverse_step(chunk)

    for copy in later_copies:
        copy.wait()
    hidden_tile = b_fc_one.shape[1]

    def out_copy(chunk):
        rows = pl.ds(chunk * back_rows, back_rows)
        return pltpu.make_async_copy(result.at[rows], out.at[rows], out_sem.at[chunk])

    @pl.loop(0, BACK_CHUNKS)
    def token_step(chunk):
        rows = pl.ds(chunk * back_rows, back_rows)
        count = back_rows * tile_cols
        lon_arrive(*home, chunk, rows)

        def gather(ref):
            return jnp.concatenate(
                [ref[block, rows].reshape(count, chans) for block in range(lon_count)], axis=1
            ).astype(jnp.float32)

        mixed = (
            gather(tokens_in)
            + gather(normed)
            + embedded[rows].reshape(count, width).astype(jnp.float32)
        ).astype(jnp.bfloat16)
        lines = norm_rows(mixed, gain_two[...], shift_two[...]).astype(jnp.bfloat16)
        total[...] = mixed.astype(jnp.float32) + b_fc_two[...]

        @pl.loop(0, b_fc_one.shape[0])
        def hidden_step(tile):
            part = pl.ds(pl.multiple_of(tile * hidden_tile, hidden_tile), hidden_tile)
            raw = dot(lines, w_fc_one_v[:, part]) + b_fc_one[pl.ds(tile, 1), :]
            hidden = (0.5 * raw * (1.0 + lax.erf(raw * math.sqrt(0.5)))).astype(jnp.bfloat16)
            total[...] += dot(hidden, w_fc_two_v[part, :])

        result[rows] = total[...].astype(jnp.bfloat16).reshape(back_rows, tile_cols, width)
        out_copy(chunk).start()

        @pl.when(chunk + AHEAD < BACK_CHUNKS)
        def inverse_rest():
            inverse_step(chunk + AHEAD)

    @pl.loop(0, FORWARD_CHUNKS)
    def front_drain(chunk):
        rows = pl.ds(chunk * fwd_rows, fwd_rows)
        sent("lon", lon_steps, lon_peer, my_lon, *front, chunk, rows)
        sent("lat", lat_steps, lat_peer, my_lat, *over, chunk, rows)

    @pl.loop(0, BACK_CHUNKS)
    def back_drain(chunk):
        rows = pl.ds(chunk * back_rows, back_rows)
        sent("lat", lat_steps, lat_peer, my_lat, *under, chunk, rows)
        sent("lon", lon_steps, lon_peer, my_lon, *home, chunk, rows)
        out_copy(chunk).wait()


def per_device_fused(
    patches,
    w_embed,
    b_embed,
    pos_embed,
    gain_one,
    shift_one,
    w_spec_one,
    b_spec_one,
    w_spec_two,
    b_spec_two,
    gain_two,
    shift_two,
    w_fc_one,
    b_fc_one,
    w_fc_two,
    b_fc_two,
):
    lat_count = lax.axis_size("lat")
    lon_count = lax.axis_size("lon")
    tile_rows, tile_cols, patch_len = patches.shape
    width = w_embed.shape[1]
    hid = w_fc_one.shape[1]
    total_rows = tile_rows * lat_count
    total_cols = tile_cols * lon_count
    wave_count = total_cols // 2
    own_waves = wave_count // lat_count
    pair = 2 * own_waves
    pitch = pair + 8
    chans = width // lon_count
    cos_w, sin_w = host_tables(total_cols, wave_count)
    cos_h, sin_h = host_tables(total_rows, total_rows)

    def by_owner(real, imag):
        shape = (lat_count, own_waves, total_cols)
        both = np.stack([real.reshape(shape), imag.reshape(shape)], axis=1)
        return both.reshape(2 * wave_count, total_cols)

    weight_k = np.where(np.arange(wave_count) == 0, 1.0, 2.0).astype(np.float32)[:, None]
    tables = [
        by_owner(cos_w, -sin_w),
        by_owner(weight_k * cos_w, -weight_k * sin_w).T,
        np.block([[cos_h, sin_h], [-sin_h, cos_h]]),
        np.block([[cos_h, -sin_h], [sin_h, cos_h]]),
    ]
    tables = [jnp.asarray(t, jnp.bfloat16) for t in tables]
    hidden_tile = 512
    vmem = pl.BlockSpec(memory_space=pltpu.VMEM)
    hbm = pl.BlockSpec(memory_space=pl.ANY)
    tile = (tile_rows, tile_cols, width)
    by_lon = (lon_count, tile_rows, tile_cols, chans)
    by_lat = (lat_count, tile_rows, pair, chans)
    bf16 = jnp.bfloat16
    dma = pltpu.SemaphoreType.DMA
    return pl.pallas_call(
        functools.partial(fused_kernel, lat_count, lon_count),
        out_shape=jax.ShapeDtypeStruct(tile, bf16),
        in_specs=[hbm, hbm, vmem, hbm, vmem, vmem, vmem, vmem, vmem, vmem, vmem, vmem]
        + [hbm, vmem, hbm, vmem, vmem, vmem, vmem, vmem],
        out_specs=hbm,
        scratch_shapes=[
            pltpu.VMEM(patches.shape, bf16),
            pltpu.VMEM(w_embed.shape, bf16),
            pltpu.VMEM(tile, bf16),
            pltpu.VMEM(w_fc_one.shape, bf16),
            pltpu.VMEM(w_fc_two.shape, bf16),
            pltpu.VMEM(tile, bf16),
            pltpu.VMEM(by_lon, bf16),
            pltpu.VMEM(by_lon, bf16),
            pltpu.VMEM(by_lat, bf16),
            pltpu.VMEM(by_lat, bf16),
            pltpu.VMEM((total_rows * pitch, chans), jnp.float32),
            pltpu.VMEM(by_lat, bf16),
            pltpu.VMEM(by_lat, bf16),
            pltpu.VMEM(by_lon, bf16),
            pltpu.VMEM(by_lon, bf16),
            pltpu.VMEM((tile_rows // BACK_CHUNKS * tile_cols, width), jnp.float32),
            pltpu.VMEM(tile, bf16),
            dma((5,)),
            dma((BACK_CHUNKS,)),
            dma((FORWARD_CHUNKS, lon_count)),
            dma((FORWARD_CHUNKS, lon_count)),
            dma((FORWARD_CHUNKS, lat_count)),
            dma((FORWARD_CHUNKS, lat_count)),
            dma((BACK_CHUNKS, lat_count)),
            dma((BACK_CHUNKS, lat_count)),
            dma((BACK_CHUNKS, lon_count)),
            dma((BACK_CHUNKS, lon_count)),
        ],
        compiler_params=pltpu.CompilerParams(
            collective_id=0, has_side_effects=True, vmem_limit_bytes=66_000_000
        ),
    )(
        patches,
        w_embed,
        b_embed.reshape(1, width),
        pos_embed,
        gain_one.reshape(1, width),
        shift_one.reshape(1, width),
        w_spec_one,
        b_spec_one,
        w_spec_two,
        b_spec_two,
        gain_two.reshape(1, width),
        shift_two.reshape(1, width),
        w_fc_one,
        b_fc_one.reshape(hid // hidden_tile, hidden_tile),
        w_fc_two,
        b_fc_two.reshape(1, width),
        *tables,
    )


def fits_fused(mesh):
    return mesh.shape["lon"] == 8 and mesh.shape["lat"] <= 4


def per_device(
    patches,
    w_embed,
    b_embed,
    pos_embed,
    gain_one,
    shift_one,
    w_spec_one,
    b_spec_one,
    w_spec_two,
    b_spec_two,
    gain_two,
    shift_two,
    w_fc_one,
    b_fc_one,
    w_fc_two,
    b_fc_two,
):
    lat_count = lax.axis_size("lat")
    lon_count = lax.axis_size("lon")
    tile_rows, tile_cols, patch_len = patches.shape
    width = w_embed.shape[1]
    total_rows = tile_rows * lat_count
    total_cols = tile_cols * lon_count
    wave_count = total_cols // 2
    own_waves = wave_count // (lat_count * lon_count)
    block_count = w_spec_one.shape[1]
    block_size = w_spec_one.shape[2]
    scale = 1.0 / math.sqrt(total_rows * total_cols)
    tokens = tile_rows * tile_cols
    flat = jnp.dot(patches.reshape(tokens, patch_len), w_embed, preferred_element_type=jnp.float32)
    embedded = (flat + b_embed + pos_embed.reshape(tokens, width).astype(jnp.float32)).astype(
        jnp.bfloat16
    )
    normed = layer_norm(embedded, gain_one, shift_one).astype(jnp.bfloat16)
    circles = lax.all_to_all(
        normed.reshape(tile_rows, tile_cols, width), "lon", split_axis=0, concat_axis=1, tiled=True
    )
    cos_w, sin_w = angle_table(total_cols, wave_count)
    fwd_cos = cos_w.T.astype(jnp.bfloat16)
    fwd_sin = (-sin_w).T.astype(jnp.bfloat16)
    lon_re = contract(circles, fwd_cos, "rwd,wk->rkd").astype(jnp.bfloat16)
    lon_im = contract(circles, fwd_sin, "rwd,wk->rkd").astype(jnp.bfloat16)
    col_re, col_im = (
        lax.all_to_all(lon_re, ("lat", "lon"), split_axis=1, concat_axis=0, tiled=True),
        lax.all_to_all(lon_im, ("lat", "lon"), split_axis=1, concat_axis=0, tiled=True),
    )
    cos_h, sin_h = angle_table(total_rows, total_rows)
    cos_h = cos_h.astype(jnp.bfloat16)
    sin_h = sin_h.astype(jnp.bfloat16)
    form = "qh,hkd->qkd"
    spec_re = (scale * (contract(cos_h, col_re, form) + contract(sin_h, col_im, form))).astype(
        jnp.bfloat16
    )
    spec_im = (scale * (contract(cos_h, col_im, form) - contract(sin_h, col_re, form))).astype(
        jnp.bfloat16
    )
    mode_shape = (total_rows * own_waves, block_count, block_size)
    mix_re, mix_im = block_mix(spec_re.reshape(mode_shape), spec_im.reshape(mode_shape), w_spec_one)
    first_re = jax.nn.relu(mix_re + b_spec_one[0]).astype(jnp.bfloat16)
    first_im = jax.nn.relu(mix_im + b_spec_one[1]).astype(jnp.bfloat16)
    mix_re, mix_im = block_mix(first_re, first_im, w_spec_two)
    shrunk_re = (
        shrink(mix_re + b_spec_two[0]).astype(jnp.bfloat16).reshape(total_rows, own_waves, width)
    )
    shrunk_im = (
        shrink(mix_im + b_spec_two[1]).astype(jnp.bfloat16).reshape(total_rows, own_waves, width)
    )
    back_re = (contract(cos_h, shrunk_re, form) - contract(sin_h, shrunk_im, form)).astype(
        jnp.bfloat16
    )
    back_im = (contract(sin_h, shrunk_re, form) + contract(cos_h, shrunk_im, form)).astype(
        jnp.bfloat16
    )
    cycle_re, cycle_im = (
        lax.all_to_all(back_re, ("lat", "lon"), split_axis=0, concat_axis=1, tiled=True),
        lax.all_to_all(back_im, ("lat", "lon"), split_axis=0, concat_axis=1, tiled=True),
    )
    weight_k = jnp.where(jnp.arange(wave_count, dtype=jnp.int32) == 0, 1.0, 2.0).astype(
        jnp.float32
    )[:, None]
    inv_cos = (weight_k * cos_w).astype(jnp.bfloat16)
    inv_sin = (weight_k * sin_w).astype(jnp.bfloat16)
    filtered = (
        scale
        * (contract(cycle_re, inv_cos, "rkd,kw->rwd") - contract(cycle_im, inv_sin, "rkd,kw->rwd"))
    ).astype(jnp.bfloat16)
    filtered = lax.all_to_all(filtered, "lon", split_axis=1, concat_axis=0, tiled=True).reshape(
        tokens, width
    )
    mixed = (
        filtered.astype(jnp.float32) + normed.astype(jnp.float32) + embedded.astype(jnp.float32)
    ).astype(jnp.bfloat16)
    normed_two = layer_norm(mixed, gain_two, shift_two).astype(jnp.bfloat16)
    hidden = jax.nn.gelu(
        jnp.dot(normed_two, w_fc_one, preferred_element_type=jnp.float32) + b_fc_one,
        approximate=False,
    ).astype(jnp.bfloat16)
    result = (
        mixed.astype(jnp.float32)
        + jnp.dot(hidden, w_fc_two, preferred_element_type=jnp.float32)
        + b_fc_two
    )
    return result.astype(jnp.bfloat16).reshape(tile_rows, tile_cols, width)


def solution(mesh):
    in_specs = (
        P("lat", "lon", None),
        P(),
        P(),
        P("lat", "lon", None),
        P(),
        P(),
        P(),
        P(),
        P(),
        P(),
        P(),
        P(),
        P(),
        P(),
        P(),
        P(),
    )
    out_specs = P("lat", "lon", None)
    body = per_device_fused if fits_fused(mesh) else per_device
    return jax.shard_map(
        body, mesh=mesh, in_specs=in_specs, out_specs=out_specs, check_vma=False
    )
```

```python
import functools
import math

import jax
import jax.numpy as jnp
import numpy as np
from jax import lax
from jax.experimental import pallas as pl
from jax.experimental.pallas import tpu as pltpu
from jax.sharding import PartitionSpec as P

MESH = pl.DeviceIdType.MESH
FORWARD_CHUNKS = 8
BACK_CHUNKS = 4
AHEAD = 3


def angle_table(length, mode_count):
    product = (
        jnp.arange(mode_count, dtype=jnp.int32)[:, None]
        * jnp.arange(length, dtype=jnp.int32)[None, :]
        % length
    )
    phase = product.astype(jnp.float32) * (2.0 * math.pi / length)
    return (jnp.cos(phase), jnp.sin(phase))


def layer_norm(values, gain_vec, shift_vec):
    floats = values.astype(jnp.float32)
    center = jnp.mean(floats, axis=-1, keepdims=True)
    spread = jnp.mean(jnp.square(floats - center), axis=-1, keepdims=True)
    return (floats - center) * lax.rsqrt(spread + 1e-06) * gain_vec + shift_vec


def shrink(values):
    return jnp.where(
        values > 0.01,
        values - 0.01,
        jnp.where(values < -0.01, values + 0.01, jnp.zeros_like(values)),
    )


def contract(table, field, form):
    return jnp.einsum(form, table, field, preferred_element_type=jnp.float32)


def block_mix(real_part, imag_part, weights):
    form = "nbi,bio->nbo"
    out_re = contract(real_part, weights[0], form) - contract(imag_part, weights[1], form)
    out_im = contract(real_part, weights[1], form) + contract(imag_part, weights[0], form)
    return (out_re, out_im)


def host_tables(length, mode_count):
    product = np.arange(mode_count)[:, None] * np.arange(length)[None, :] % length
    phase = product.astype(np.float32) * np.float32(2.0 * math.pi / length)
    return (np.cos(phase).astype(np.float32), np.sin(phase).astype(np.float32))


def norm_rows(values, gain_row, shift_row):
    floats = values.astype(jnp.float32)
    center = jnp.mean(floats, axis=-1, keepdims=True)
    floats = floats - center
    spread = jnp.mean(floats * floats, axis=-1, keepdims=True)
    return floats * lax.rsqrt(spread + 1e-06) * gain_row + shift_row


def dot(left, right):
    return jnp.dot(left, right, preferred_element_type=jnp.float32)


def fused_kernel(
    lat_count,
    lon_count,
    patches,
    w_embed,
    b_embed,
    pos_embed,
    gain_one,
    shift_one,
    w_spec_one,
    b_spec_one,
    w_spec_two,
    b_spec_two,
    gain_two,
    shift_two,
    w_fc_one,
    b_fc_one,
    w_fc_two,
    b_fc_two,
    lon_table,
    lon_back,
    lat_table,
    lat_back,
    out,
    patches_v,
    w_embed_v,
    pos_v,
    w_fc_one_v,
    w_fc_two_v,
    embedded,
    normed,
    circles,
    waves,
    columns,
    modes,
    back,
    cycles,
    filtered,
    tokens_in,
    total,
    result,
    in_sem,
    out_sem,
    s1,
    r1,
    s2,
    r2,
    s3,
    r3,
    s4,
    r4,
):
    tile_rows, tile_cols, patch_len = patches_v.shape
    width = w_embed_v.shape[1]
    chans = circles.shape[3]
    total_rows = tile_rows * lat_count
    total_cols = tile_cols * lon_count
    pair = columns.shape[2]
    own_waves = pair // 2
    pitch = modes.shape[0] // total_rows
    scale = 1.0 / math.sqrt(total_rows * total_cols)
    my_lat = lax.axis_index("lat")
    my_lon = lax.axis_index("lon")
    half = lon_count // 2
    lon_steps = sorted(range(1, lon_count), key=lambda d: abs(d - half))
    lat_steps = list(range(1, lat_count))

    def lon_peer(step):
        return lax.rem(my_lon + step, lon_count)

    def lat_peer(step):
        return lax.rem(my_lat + step, lat_count)

    def fetch(source, target, index):
        return pltpu.make_async_copy(source, target, in_sem.at[index])

    lead = pl.ds(0, tile_rows // FORWARD_CHUNKS)
    rest = pl.ds(tile_rows // FORWARD_CHUNKS, tile_rows - tile_rows // FORWARD_CHUNKS)
    first_copies = [
        fetch(w_embed, w_embed_v, 0),
        fetch(patches.at[lead], patches_v.at[lead], 1),
        fetch(pos_embed.at[lead], pos_v.at[lead], 2),
    ]
    second_copies = [
        fetch(patches.at[rest], patches_v.at[rest], 5),
        fetch(pos_embed.at[rest], pos_v.at[rest], 6),
    ]
    later_copies = [fetch(w_fc_one, w_fc_one_v, 3), fetch(w_fc_two, w_fc_two_v, 4)]
    for copy in first_copies + second_copies:
        copy.start()

    barrier = pltpu.get_barrier_semaphore()
    for step in lon_steps:
        pl.semaphore_signal(
            barrier, inc=1, device_id={"lon": lon_peer(step)}, device_id_type=MESH
        )
    for step in lat_steps:
        pl.semaphore_signal(
            barrier, inc=1, device_id={"lat": lat_peer(step)}, device_id_type=MESH
        )
    pl.semaphore_wait(barrier, lon_count + lat_count - 2)

    def exchange(axis, send, recv, send_sem, recv_sem, chunk, rows, peer, mine):
        return pltpu.make_async_remote_copy(
            src_ref=send.at[peer, rows],
            dst_ref=recv.at[mine, rows],
            send_sem=send_sem.at[chunk, peer],
            recv_sem=recv_sem.at[chunk, mine],
            device_id={axis: peer},
            device_id_type=MESH,
        )

    def lon_send(send, recv, send_sem, recv_sem, chunk, rows):
        for step in lon_steps:
            exchange(
                "lon", send, recv, send_sem, recv_sem, chunk, rows, lon_peer(step), my_lon
            ).start()

    def lat_send(send, recv, send_sem, recv_sem, chunk, rows):
        for step in lat_steps:
            exchange(
                "lat", send, recv, send_sem, recv_sem, chunk, rows, lat_peer(step), my_lat
            ).start()

    def lon_arrive(send, recv, send_sem, recv_sem, chunk, rows):
        for step in lon_steps:
            peer = lon_peer(step)
            exchange("lon", send, recv, send_sem, recv_sem, chunk, rows, peer, peer).wait_recv()

    def lat_arrive(send, recv, send_sem, recv_sem, chunk, rows):
        for step in lat_steps:
            peer = lat_peer(step)
            exchange("lat", send, recv, send_sem, recv_sem, chunk, rows, peer, peer).wait_recv()

    def sent(axis, steps, peer_of, mine, send, recv, send_sem, recv_sem, chunk, rows):
        for step in steps:
            exchange(
                axis, send, recv, send_sem, recv_sem, chunk, rows, peer_of(step), mine
            ).wait_send()

    front = (normed, circles, s1, r1)
    over = (waves, columns, s2, r2)
    under = (back, cycles, s3, r3)
    home = (filtered, tokens_in, s4, r4)
    fwd_rows = tile_rows // FORWARD_CHUNKS
    back_rows = tile_rows // BACK_CHUNKS

    for copy in first_copies:
        copy.wait()

    def embed_step(chunk):
        rows = pl.ds(chunk * fwd_rows, fwd_rows)
        count = fwd_rows * tile_cols
        flat = dot(patches_v[rows].reshape(count, patch_len), w_embed_v[...])
        flat = flat + b_embed[...] + pos_v[rows].reshape(count, width).astype(jnp.float32)
        rounded = flat.astype(jnp.bfloat16)
        embedded[rows] = rounded.reshape(fwd_rows, tile_cols, width)
        scaled = norm_rows(rounded, gain_one[...], shift_one[...]).astype(jnp.bfloat16)
        for block in range(lon_count):
            piece = scaled[:, block * chans : (block + 1) * chans]
            normed[block, rows] = piece.reshape(fwd_rows, tile_cols, chans)
        lon_send(*front, chunk, rows)
        circles[my_lon, rows] = normed[my_lon, rows]

    embed_step(0)
    for copy in second_copies:
        copy.wait()
    for copy in later_copies:
        copy.start()

    @pl.loop(1, FORWARD_CHUNKS)
    def embed_rest(chunk):
        embed_step(chunk)

    def widen_step(chunk):
        rows = pl.ds(chunk * fwd_rows, fwd_rows)
        lat_arrive(*over, chunk, rows)
        for owner in range(lat_count):
            for row in range(fwd_rows):
                place = (owner * tile_rows + chunk * fwd_rows + row) * pitch
                modes[pl.ds(pl.multiple_of(place, 8), pair), :] = columns[
                    owner, chunk * fwd_rows + row
                ].astype(jnp.float32)

    @pl.loop(0, FORWARD_CHUNKS)
    def wave_step(chunk):
        rows = pl.ds(chunk * fwd_rows, fwd_rows)
        lon_arrive(*front, chunk, rows)
        for row in range(0, fwd_rows, 2):
            base = chunk * fwd_rows + row
            field = jnp.concatenate(
                [circles[:, base + i].reshape(total_cols, chans) for i in range(2)], axis=1
            )
            spectrum = dot(lon_table[...], field).astype(jnp.bfloat16)
            for owner in range(lat_count):
                for i in range(2):
                    waves[owner, base + i] = spectrum[
                        owner * pair : (owner + 1) * pair, i * chans : (i + 1) * chans
                    ]
        lat_send(*over, chunk, rows)
        columns[my_lat, rows] = waves[my_lat, rows]

        @pl.when(chunk > 0)
        def widen_previous():
            widen_step(chunk - 1)

    widen_step(FORWARD_CHUNKS - 1)

    def mix_matrix(weights):
        real, imag = weights[0, my_lon], weights[1, my_lon]
        return jnp.concatenate(
            [
                jnp.concatenate([real, imag], axis=1),
                jnp.concatenate([-imag, real], axis=1),
            ],
            axis=0,
        )

    def mix_bias(bias):
        return jnp.concatenate(
            [bias[0, pl.ds(my_lon, 1), :], bias[1, pl.ds(my_lon, 1), :]], axis=1
        )

    mix_one, mix_two = mix_matrix(w_spec_one), mix_matrix(w_spec_two)
    bias_one, bias_two = mix_bias(b_spec_one), mix_bias(b_spec_two)
    group = 8

    @pl.loop(0, own_waves // group)
    def mode_step(step):
        def place(i, part):
            return pl.ds(step * group + i + part * own_waves, total_rows, stride=pitch)

        field = jnp.concatenate(
            [
                jnp.concatenate([modes[place(i, 0), :], modes[place(i, 1), :]], axis=0).astype(
                    jnp.bfloat16
                )
                for i in range(group)
            ],
            axis=1,
        )
        spec = (scale * dot(lat_table[...], field)).astype(jnp.bfloat16)
        stacked = jnp.concatenate(
            [
                jnp.concatenate(
                    [
                        spec[:total_rows, i * chans : (i + 1) * chans],
                        spec[total_rows:, i * chans : (i + 1) * chans],
                    ],
                    axis=1,
                )
                for i in range(group)
            ],
            axis=0,
        )
        first = jnp.maximum(dot(stacked, mix_one) + bias_one, 0.0).astype(jnp.bfloat16)
        second = shrink(dot(first, mix_two) + bias_two).astype(jnp.bfloat16)
        turned = jnp.concatenate(
            [
                jnp.concatenate(
                    [
                        second[i * total_rows : (i + 1) * total_rows, :chans],
                        second[i * total_rows : (i + 1) * total_rows, chans:],
                    ],
                    axis=0,
                )
                for i in range(group)
            ],
            axis=1,
        )
        returned = dot(lat_back[...], turned)
        for i in range(group):
            modes[place(i, 0), :] = returned[:total_rows, i * chans : (i + 1) * chans]
            modes[place(i, 1), :] = returned[total_rows:, i * chans : (i + 1) * chans]

    @pl.loop(0, BACK_CHUNKS)
    def return_step(chunk):
        rows = pl.ds(chunk * back_rows, back_rows)
        for owner in range(lat_count):
            for row in range(back_rows):
                place = (owner * tile_rows + chunk * back_rows + row) * pitch
                back[owner, chunk * back_rows + row] = modes[
                    pl.ds(pl.multiple_of(place, 8), pair), :
                ].astype(jnp.bfloat16)
        lat_send(*under, chunk, rows)
        cycles[my_lat, rows] = back[my_lat, rows]

    def inverse_step(chunk):
        rows = pl.ds(chunk * back_rows, back_rows)
        lat_arrive(*under, chunk, rows)
        for row in range(0, back_rows, 2):
            base = chunk * back_rows + row
            field = jnp.concatenate(
                [cycles[:, base + i].reshape(lat_count * pair, chans) for i in range(2)], axis=1
            )
            values = (scale * dot(lon_back[...], field)).astype(jnp.bfloat16)
            for owner in range(lon_count):
                for i in range(2):
                    filtered[owner, base + i] = values[
                        owner * tile_cols : (owner + 1) * tile_cols, i * chans : (i + 1) * chans
                    ]
        lon_send(*home, chunk, rows)
        tokens_in[my_lon, rows] = filtered[my_lon, rows]

    @pl.loop(0, AHEAD)
    def inverse_ahead(chunk):
        inverse_step(chunk)

    for copy in later_copies:
        copy.wait()
    hidden_tile = b_fc_one.shape[1]

    def out_copy(chunk):
        rows = pl.ds(chunk * back_rows, back_rows)
        return pltpu.make_async_copy(result.at[rows], out.at[rows], out_sem.at[chunk])

    @pl.loop(0, BACK_CHUNKS)
    def token_step(chunk):
        rows = pl.ds(chunk * back_rows, back_rows)
        count = back_rows * tile_cols
        lon_arrive(*home, chunk, rows)

        def gather(ref):
            return jnp.concatenate(
                [ref[block, rows].reshape(count, chans) for block in range(lon_count)], axis=1
            ).astype(jnp.float32)

        mixed = (
            gather(tokens_in)
            + gather(normed)
            + embedded[rows].reshape(count, width).astype(jnp.float32)
        ).astype(jnp.bfloat16)
        lines = norm_rows(mixed, gain_two[...], shift_two[...]).astype(jnp.bfloat16)
        total[...] = mixed.astype(jnp.float32) + b_fc_two[...]

        @pl.loop(0, b_fc_one.shape[0])
        def hidden_step(tile):
            part = pl.ds(pl.multiple_of(tile * hidden_tile, hidden_tile), hidden_tile)
            raw = dot(lines, w_fc_one_v[:, part]) + b_fc_one[pl.ds(tile, 1), :]
            hidden = (0.5 * raw * (1.0 + lax.erf(raw * math.sqrt(0.5)))).astype(jnp.bfloat16)
            total[...] += dot(hidden, w_fc_two_v[part, :])

        result[rows] = total[...].astype(jnp.bfloat16).reshape(back_rows, tile_cols, width)
        out_copy(chunk).start()

        @pl.when(chunk + AHEAD < BACK_CHUNKS)
        def inverse_rest():
            inverse_step(chunk + AHEAD)

    @pl.loop(0, FORWARD_CHUNKS)
    def front_drain(chunk):
        rows = pl.ds(chunk * fwd_rows, fwd_rows)
        sent("lon", lon_steps, lon_peer, my_lon, *front, chunk, rows)
        sent("lat", lat_steps, lat_peer, my_lat, *over, chunk, rows)

    @pl.loop(0, BACK_CHUNKS)
    def back_drain(chunk):
        rows = pl.ds(chunk * back_rows, back_rows)
        sent("lat", lat_steps, lat_peer, my_lat, *under, chunk, rows)
        sent("lon", lon_steps, lon_peer, my_lon, *home, chunk, rows)
        out_copy(chunk).wait()


def per_device_fused(
    patches,
    w_embed,
    b_embed,
    pos_embed,
    gain_one,
    shift_one,
    w_spec_one,
    b_spec_one,
    w_spec_two,
    b_spec_two,
    gain_two,
    shift_two,
    w_fc_one,
    b_fc_one,
    w_fc_two,
    b_fc_two,
):
    lat_count = lax.axis_size("lat")
    lon_count = lax.axis_size("lon")
    tile_rows, tile_cols, patch_len = patches.shape
    width = w_embed.shape[1]
    hid = w_fc_one.shape[1]
    total_rows = tile_rows * lat_count
    total_cols = tile_cols * lon_count
    wave_count = total_cols // 2
    own_waves = wave_count // lat_count
    pair = 2 * own_waves
    pitch = pair + 8
    chans = width // lon_count
    cos_w, sin_w = host_tables(total_cols, wave_count)
    cos_h, sin_h = host_tables(total_rows, total_rows)

    def by_owner(real, imag):
        shape = (lat_count, own_waves, total_cols)
        both = np.stack([real.reshape(shape), imag.reshape(shape)], axis=1)
        return both.reshape(2 * wave_count, total_cols)

    weight_k = np.where(np.arange(wave_count) == 0, 1.0, 2.0).astype(np.float32)[:, None]
    tables = [
        by_owner(cos_w, -sin_w),
        by_owner(weight_k * cos_w, -weight_k * sin_w).T,
        np.block([[cos_h, sin_h], [-sin_h, cos_h]]),
        np.block([[cos_h, -sin_h], [sin_h, cos_h]]),
    ]
    tables = [jnp.asarray(t, jnp.bfloat16) for t in tables]
    hidden_tile = 512
    vmem = pl.BlockSpec(memory_space=pltpu.VMEM)
    hbm = pl.BlockSpec(memory_space=pl.ANY)
    tile = (tile_rows, tile_cols, width)
    by_lon = (lon_count, tile_rows, tile_cols, chans)
    by_lat = (lat_count, tile_rows, pair, chans)
    bf16 = jnp.bfloat16
    dma = pltpu.SemaphoreType.DMA
    return pl.pallas_call(
        functools.partial(fused_kernel, lat_count, lon_count),
        out_shape=jax.ShapeDtypeStruct(tile, bf16),
        in_specs=[hbm, hbm, vmem, hbm, vmem, vmem, vmem, vmem, vmem, vmem, vmem, vmem]
        + [hbm, vmem, hbm, vmem, vmem, vmem, vmem, vmem],
        out_specs=hbm,
        scratch_shapes=[
            pltpu.VMEM(patches.shape, bf16),
            pltpu.VMEM(w_embed.shape, bf16),
            pltpu.VMEM(tile, bf16),
            pltpu.VMEM(w_fc_one.shape, bf16),
            pltpu.VMEM(w_fc_two.shape, bf16),
            pltpu.VMEM(tile, bf16),
            pltpu.VMEM(by_lon, bf16),
            pltpu.VMEM(by_lon, bf16),
            pltpu.VMEM(by_lat, bf16),
            pltpu.VMEM(by_lat, bf16),
            pltpu.VMEM((total_rows * pitch, chans), jnp.float32),
            pltpu.VMEM(by_lat, bf16),
            pltpu.VMEM(by_lat, bf16),
            pltpu.VMEM(by_lon, bf16),
            pltpu.VMEM(by_lon, bf16),
            pltpu.VMEM((tile_rows // BACK_CHUNKS * tile_cols, width), jnp.float32),
            pltpu.VMEM(tile, bf16),
            dma((7,)),
            dma((BACK_CHUNKS,)),
            dma((FORWARD_CHUNKS, lon_count)),
            dma((FORWARD_CHUNKS, lon_count)),
            dma((FORWARD_CHUNKS, lat_count)),
            dma((FORWARD_CHUNKS, lat_count)),
            dma((BACK_CHUNKS, lat_count)),
            dma((BACK_CHUNKS, lat_count)),
            dma((BACK_CHUNKS, lon_count)),
            dma((BACK_CHUNKS, lon_count)),
        ],
        compiler_params=pltpu.CompilerParams(
            collective_id=0, has_side_effects=True, vmem_limit_bytes=66_000_000
        ),
    )(
        patches,
        w_embed,
        b_embed.reshape(1, width),
        pos_embed,
        gain_one.reshape(1, width),
        shift_one.reshape(1, width),
        w_spec_one,
        b_spec_one,
        w_spec_two,
        b_spec_two,
        gain_two.reshape(1, width),
        shift_two.reshape(1, width),
        w_fc_one,
        b_fc_one.reshape(hid // hidden_tile, hidden_tile),
        w_fc_two,
        b_fc_two.reshape(1, width),
        *tables,
    )


def fits_fused(mesh):
    return mesh.shape["lon"] == 8 and mesh.shape["lat"] <= 4


def per_device(
    patches,
    w_embed,
    b_embed,
    pos_embed,
    gain_one,
    shift_one,
    w_spec_one,
    b_spec_one,
    w_spec_two,
    b_spec_two,
    gain_two,
    shift_two,
    w_fc_one,
    b_fc_one,
    w_fc_two,
    b_fc_two,
):
    lat_count = lax.axis_size("lat")
    lon_count = lax.axis_size("lon")
    tile_rows, tile_cols, patch_len = patches.shape
    width = w_embed.shape[1]
    total_rows = tile_rows * lat_count
    total_cols = tile_cols * lon_count
    wave_count = total_cols // 2
    own_waves = wave_count // (lat_count * lon_count)
    block_count = w_spec_one.shape[1]
    block_size = w_spec_one.shape[2]
    scale = 1.0 / math.sqrt(total_rows * total_cols)
    tokens = tile_rows * tile_cols
    flat = jnp.dot(patches.reshape(tokens, patch_len), w_embed, preferred_element_type=jnp.float32)
    embedded = (flat + b_embed + pos_embed.reshape(tokens, width).astype(jnp.float32)).astype(
        jnp.bfloat16
    )
    normed = layer_norm(embedded, gain_one, shift_one).astype(jnp.bfloat16)
    circles = lax.all_to_all(
        normed.reshape(tile_rows, tile_cols, width), "lon", split_axis=0, concat_axis=1, tiled=True
    )
    cos_w, sin_w = angle_table(total_cols, wave_count)
    fwd_cos = cos_w.T.astype(jnp.bfloat16)
    fwd_sin = (-sin_w).T.astype(jnp.bfloat16)
    lon_re = contract(circles, fwd_cos, "rwd,wk->rkd").astype(jnp.bfloat16)
    lon_im = contract(circles, fwd_sin, "rwd,wk->rkd").astype(jnp.bfloat16)
    col_re, col_im = (
        lax.all_to_all(lon_re, ("lat", "lon"), split_axis=1, concat_axis=0, tiled=True),
        lax.all_to_all(lon_im, ("lat", "lon"), split_axis=1, concat_axis=0, tiled=True),
    )
    cos_h, sin_h = angle_table(total_rows, total_rows)
    cos_h = cos_h.astype(jnp.bfloat16)
    sin_h = sin_h.astype(jnp.bfloat16)
    form = "qh,hkd->qkd"
    spec_re = (scale * (contract(cos_h, col_re, form) + contract(sin_h, col_im, form))).astype(
        jnp.bfloat16
    )
    spec_im = (scale * (contract(cos_h, col_im, form) - contract(sin_h, col_re, form))).astype(
        jnp.bfloat16
    )
    mode_shape = (total_rows * own_waves, block_count, block_size)
    mix_re, mix_im = block_mix(spec_re.reshape(mode_shape), spec_im.reshape(mode_shape), w_spec_one)
    first_re = jax.nn.relu(mix_re + b_spec_one[0]).astype(jnp.bfloat16)
    first_im = jax.nn.relu(mix_im + b_spec_one[1]).astype(jnp.bfloat16)
    mix_re, mix_im = block_mix(first_re, first_im, w_spec_two)
    shrunk_re = (
        shrink(mix_re + b_spec_two[0]).astype(jnp.bfloat16).reshape(total_rows, own_waves, width)
    )
    shrunk_im = (
        shrink(mix_im + b_spec_two[1]).astype(jnp.bfloat16).reshape(total_rows, own_waves, width)
    )
    back_re = (contract(cos_h, shrunk_re, form) - contract(sin_h, shrunk_im, form)).astype(
        jnp.bfloat16
    )
    back_im = (contract(sin_h, shrunk_re, form) + contract(cos_h, shrunk_im, form)).astype(
        jnp.bfloat16
    )
    cycle_re, cycle_im = (
        lax.all_to_all(back_re, ("lat", "lon"), split_axis=0, concat_axis=1, tiled=True),
        lax.all_to_all(back_im, ("lat", "lon"), split_axis=0, concat_axis=1, tiled=True),
    )
    weight_k = jnp.where(jnp.arange(wave_count, dtype=jnp.int32) == 0, 1.0, 2.0).astype(
        jnp.float32
    )[:, None]
    inv_cos = (weight_k * cos_w).astype(jnp.bfloat16)
    inv_sin = (weight_k * sin_w).astype(jnp.bfloat16)
    filtered = (
        scale
        * (contract(cycle_re, inv_cos, "rkd,kw->rwd") - contract(cycle_im, inv_sin, "rkd,kw->rwd"))
    ).astype(jnp.bfloat16)
    filtered = lax.all_to_all(filtered, "lon", split_axis=1, concat_axis=0, tiled=True).reshape(
        tokens, width
    )
    mixed = (
        filtered.astype(jnp.float32) + normed.astype(jnp.float32) + embedded.astype(jnp.float32)
    ).astype(jnp.bfloat16)
    normed_two = layer_norm(mixed, gain_two, shift_two).astype(jnp.bfloat16)
    hidden = jax.nn.gelu(
        jnp.dot(normed_two, w_fc_one, preferred_element_type=jnp.float32) + b_fc_one,
        approximate=False,
    ).astype(jnp.bfloat16)
    result = (
        mixed.astype(jnp.float32)
        + jnp.dot(hidden, w_fc_two, preferred_element_type=jnp.float32)
        + b_fc_two
    )
    return result.astype(jnp.bfloat16).reshape(tile_rows, tile_cols, width)


def solution(mesh):
    in_specs = (
        P("lat", "lon", None),
        P(),
        P(),
        P("lat", "lon", None),
        P(),
        P(),
        P(),
        P(),
        P(),
        P(),
        P(),
        P(),
        P(),
        P(),
        P(),
        P(),
    )
    out_specs = P("lat", "lon", None)
    body = per_device_fused if fits_fused(mesh) else per_device
    return jax.shard_map(
        body, mesh=mesh, in_specs=in_specs, out_specs=out_specs, check_vma=False
    )
```
